128 devices in a mesh: row: 8 (over y, core), col: 16 (over x, z).
Axes of the slice: x: 4, y: 4, z: 4, core: 2. Of those that a mesh axis runs over, the one named last changes fastest.
Arguments:
- object_amp: float32 [4, 4096, 8192], P(None, 'row', 'col'), may hold values from 0.5 to 1.5
- object_phase: float32 [4, 4096, 8192], P(None, 'row', 'col'), may hold values from -3.140625 to 3.140625
- probe_field: float32 [2, 256, 256], replicated, may hold values from -5 to 5
- measured: float32 [8, 16, 4, 256, 256], P('row', 'col'), may hold values from 0 to 2
- offsets: int32 [8, 16, 4, 2], P('row', 'col'), may hold values from 0 to 512
- counts: int32 [8, 16], P('row', 'col'), may hold values from 1 to 4, as said below
Outputs:
- new_real: float32 [4, 4096, 8192], P(None, 'row', 'col')
- new_imag: float32 [4, 4096, 8192], P(None, 'row', 'col')
The draws below stay inside these ranges and needn't reach their ends.
Inputs may be any that keep to these rules, and one draw needn't show every extreme that they name: `counts`: every count is at least one, and some tile uses all 4 slots. Slots at or beyond a tile's count are unused. `offsets`: entries of unused slots carry no meaning.
All inputs are finite; a program needn't handle non-finite values.
Results may differ from the reference program's by a relative error of at most 0.0003.
Values sent between devices are 32-bit elements; how exact they have to be, the bound alone decides.
No kernel may reach another device: no remote copies, remote signals or barrier semaphores. Data moves between devices by JAX's collectives and lax.ppermute only.
A program may use at most 192 MiB of HBM per device.

```python
import jax
import jax.numpy as jnp
from jax import lax

P_SIZE = 256
SL = 4
MAXPOS = 4
TILE = 512
TROWS = 8
TCOLS = 16
ROWS = 4096
COLS = 8192


def draw_counts(key, part):
    first_key, second_key, third_key = jax.random.split(jax.random.fold_in(key, 17), 3)
    first = jax.random.randint(first_key, (TROWS, TCOLS), 0, 3)
    second = jax.random.randint(second_key, (TROWS, TCOLS), 0, 3)
    base = jnp.minimum(1 + first + second, MAXPOS)
    chosen = jax.random.randint(third_key, (), 0, TROWS * TCOLS)
    flat_counts = base.reshape(-1)
    flat_counts = jnp.where(jnp.arange(TROWS * TCOLS) == chosen, MAXPOS, flat_counts)
    return flat_counts.reshape(TROWS, TCOLS).astype(jnp.int32)


def touch_ends(entries, own_key, low, top_value):
    shape = entries.shape
    place = [jax.random.randint(jax.random.fold_in(own_key, axis), (), 0, shape[axis]) for axis in range(len(shape))]
    entries = entries.at[tuple(place)].set(low)
    longest = shape.index(max(shape))
    place[longest] = (place[longest] + 1) % shape[longest]
    return entries.at[tuple(place)].set(top_value)


def level_of(rng, extent, cuts, low, top_value):
    factor_of = 1.0
    for axis_at, blocks in cuts:
        steps = jax.random.uniform(jax.random.fold_in(jax.random.fold_in(rng, 6), axis_at), (blocks,), jnp.float32, low / len(cuts), top_value / len(cuts))
        factor_of = factor_of * jnp.repeat(jnp.exp(steps), extent[axis_at] // blocks).reshape((-1,) + (1,) * (len(extent) - 1 - axis_at))
    return factor_of


def bell_draw(rng, shape, scale, limit, kind=jnp.bfloat16):
    drawn = jax.random.normal(rng, shape, jnp.float32) * scale
    return jnp.minimum(jnp.maximum(drawn, -limit), limit).astype(kind)


def setup_inputs(seed: int = 0) -> dict:
    key_list = jax.random.split(jax.random.key(seed), 7)
    return {
        "object_amp": jnp.clip(1.0 + 0.1 * jax.random.normal(key_list[0], (SL, ROWS, COLS), jnp.float32), 0.5, 1.5),
        "object_phase": jnp.clip(jax.random.uniform(key_list[1], (SL, ROWS, COLS), jnp.float32, -3.140625, 3.140625), -3.140625, 3.140625),
        "probe_field": bell_draw(key_list[2], (2, P_SIZE, P_SIZE), 0.7, 5.0, jnp.float32),
        "measured": jnp.clip(2.0 * jax.random.uniform(key_list[3], (TROWS, TCOLS, MAXPOS, P_SIZE, P_SIZE), jnp.float32) ** level_of(key_list[3], (TROWS, TCOLS, MAXPOS, P_SIZE, P_SIZE), ((0, 8), (1, 16)), -0.2, 0.2), 0.0, 2.0),
        "offsets": touch_ends(jax.random.randint(key_list[4], (TROWS, TCOLS, MAXPOS, 2), 0, TILE + 1), jax.random.fold_in(key_list[4], 1), 0, TILE).astype(jnp.int32),
        "counts": draw_counts(jax.random.fold_in(key_list[6], 71), 0),
    }


FRESNEL = 0.0005


def forward_fft(field):
    return jnp.fft.fft2(field, norm="ortho")


def inverse_fft(field):
    return jnp.fft.ifft2(field, norm="ortho")


def position_terms(window, target, probe_wave, kernel):
    wave = probe_wave
    incident = []
    exit_wave = wave
    for layer in range(SL):
        incident.append(wave)
        exit_wave = wave * window[layer]
        if layer + 1 < SL:
            wave = inverse_fft(forward_fft(exit_wave) * kernel)
    far = forward_fft(exit_wave)
    misfit = far.real * far.real + far.imag * far.imag - target
    back = inverse_fft(misfit * far)
    grads = [None] * SL
    lights = [None] * SL
    for layer in reversed(range(SL)):
        here = incident[layer]
        grads[layer] = jnp.conj(here) * back
        lights[layer] = here.real * here.real + here.imag * here.imag
        if layer > 0:
            back = inverse_fft(forward_fft(jnp.conj(window[layer]) * back) * jnp.conj(kernel))
    return jnp.stack(grads), jnp.stack(lights)


def reference(object_amp, object_phase, probe_field, measured, offsets, counts):
    width = P_SIZE // 2
    slab = lax.complex(object_amp * jnp.cos(object_phase), object_amp * jnp.sin(object_phase))
    padded = jnp.pad(slab, ((0, 0), (width, width), (width, width)))
    probe_wave = lax.complex(probe_field[0], probe_field[1])
    counter = jnp.arange(P_SIZE, dtype=jnp.int32)
    frequency = (((counter + P_SIZE // 2) % P_SIZE) - P_SIZE // 2).astype(jnp.float32)
    phases = FRESNEL * (frequency[:, None] ** 2 + frequency[None, :] ** 2)
    kernel = lax.complex(jnp.cos(phases), jnp.sin(phases))
    slot_total = TROWS * TCOLS * MAXPOS
    order_ids = jnp.arange(slot_total, dtype=jnp.int32)
    tile_row = order_ids // (TCOLS * MAXPOS)
    tile_col = (order_ids // MAXPOS) % TCOLS
    slot_ids = order_ids % MAXPOS
    live = (slot_ids < counts[tile_row, tile_col]).astype(jnp.float32)
    tops = (tile_row * TILE + offsets[tile_row, tile_col, slot_ids, 0]).astype(jnp.int32)
    lefts = (tile_col * TILE + offsets[tile_row, tile_col, slot_ids, 1]).astype(jnp.int32)
    flat_measured = measured.reshape(slot_total, P_SIZE, P_SIZE)
    grad_start = jnp.zeros(padded.shape, dtype=padded.dtype)
    light_start = jnp.zeros(padded.shape, dtype=object_amp.dtype)

    def visit(carry, item):
        grad_total, light_total = carry
        top, left, weight, target = item
        start = (jnp.int32(0), top.astype(jnp.int32), left.astype(jnp.int32))
        window = lax.dynamic_slice(padded, start, (SL, P_SIZE, P_SIZE))
        grads, lights = position_terms(window, target, probe_wave, kernel)
        grad_total = lax.dynamic_update_slice(grad_total, lax.dynamic_slice(grad_total, start, (SL, P_SIZE, P_SIZE)) + weight * grads, start)
        light_total = lax.dynamic_update_slice(light_total, lax.dynamic_slice(light_total, start, (SL, P_SIZE, P_SIZE)) + weight * lights, start)
        return (grad_total, light_total), None

    (grad_total, light_total), _ = lax.scan(visit, (grad_start, light_start), (tops, lefts, live, flat_measured))
    grad_total = grad_total[:, width:width + ROWS, width:width + COLS]
    light_total = light_total[:, width:width + ROWS, width:width + COLS]
    updated = slab - grad_total / (light_total + 1.0)
    return updated.real, updated.imag
```

```python
import functools

import jax
import jax.numpy as jnp
import numpy as np
from jax import lax
from jax.experimental import pallas as pl
from jax.experimental.pallas import tpu as pltpu
from jax.sharding import PartitionSpec as P

FRESNEL = 0.0005
N = 256
H = 128
SLICES = 4
SLOTS = 4
TILE = 512
F32 = jnp.float32
BF16 = jnp.bfloat16
CHUNKS = ((0, 1), (2,), (3,))

SEGMENTS = ((0, H, 0, H), (1, 0, H, N), (2, 0, H + N, H))


def real_form(matrix):
    return np.block([[matrix.real, -matrix.imag], [matrix.imag, matrix.real]])


def split_table(pair):
    parts = np.stack([real_form(m) for m in pair]).astype(np.float32)
    high = parts.astype(BF16)
    low = (parts - high.astype(np.float32)).astype(BF16)
    return np.stack([high, low])


def tables():
    counter = np.arange(N)
    frequency = (counter + H) % N - H
    q = np.exp(1j * FRESNEL * frequency.astype(np.float64) ** 2)
    spread = np.fft.ifft(q)
    j, m = np.arange(H)[:, None], np.arange(H)[None, :]
    near, far = spread[(j - m) % N], spread[(j - m - H) % N]
    prop = ((near + far) / 2, (near - far) / 2)
    even = np.exp(-2j * np.pi * ((j * m) % H) / H) / 16
    odd = np.exp(-2j * np.pi * ((m * (2 * j + 1)) % N) / N) / 16
    prop_table, dft_table = split_table(prop), split_table((even, odd))
    return (
        prop_table,
        np.ascontiguousarray(prop_table.swapaxes(-1, -2)),
        dft_table,
        np.ascontiguousarray(dft_table.swapaxes(-1, -2)),
    )


def fit_sincos():
    u = np.cos(np.linspace(0, np.pi, 4001)) * 0.79
    w = u * u
    sin_part = np.polynomial.polynomial.polyfit(w, np.where(u == 0, 1.0, np.sin(u) / np.where(u == 0, 1.0, u)), 4)
    cos_part = np.polynomial.polynomial.polyfit(w, np.cos(u), 4)
    return [float(c) for c in sin_part], [float(c) for c in cos_part]


SIN_PART, COS_PART = fit_sincos()


def poly(w, coefficients):
    total = jnp.full_like(w, coefficients[-1])
    for c in coefficients[-2::-1]:
        total = total * w + c
    return total


def sincos(phase):
    u = phase * 0.25
    w = u * u
    s, c = u * poly(w, SIN_PART), poly(w, COS_PART)
    s, c = 2.0 * s * c, 1.0 - 2.0 * s * s
    return 2.0 * s * c, 1.0 - 2.0 * s * s


def split(x):
    high = x.astype(BF16)
    return high, (x - high.astype(F32)).astype(BF16)


def dot(a, b):
    return jnp.dot(a, b, preferred_element_type=F32)


def left_product(table, which, z):
    zh, zl = split(z)
    mh, ml = table[0, which], table[1, which]
    return dot(mh, zh) + dot(ml, zh) + dot(mh, zl)


def right_product(table, which, z):
    zh, zl = split(z)
    mh, ml = table[0, which], table[1, which]
    return dot(zh, mh) + dot(zh, ml) + dot(zl, mh)


def halves(x, axis):
    return (x[:H], x[H:]) if axis == 0 else (x[:, :H], x[:, H:])


def along(wave, axis, table, before, after):
    (r0, r1), (i0, i1) = halves(wave[0], axis), halves(wave[1], axis)
    if before:
        r0, r1, i0, i1 = r0 + r1, r0 - r1, i0 + i1, i0 - i1
    product = left_product if axis == 0 else right_product
    first = product(table, 0, jnp.concatenate([r0, i0], axis))
    second = product(table, 1, jnp.concatenate([r1, i1], axis))
    (r0, i0), (r1, i1) = halves(first, axis), halves(second, axis)
    if after:
        r0, r1, i0, i1 = r0 + r1, r0 - r1, i0 + i1, i0 - i1
    return jnp.concatenate([r0, r1], axis), jnp.concatenate([i0, i1], axis)


def both_axes(wave, left, right, before, after):
    wave = along(wave, 0, left, before, after)
    return along(wave, 1, right, before, after)


def product_of(a, b):
    return a[0] * b[0] - a[1] * b[1], a[0] * b[1] + a[1] * b[0]


def conj_product(a, b):
    return a[0] * b[0] + a[1] * b[1], a[0] * b[1] - a[1] * b[0]


class Place:
    def __init__(self, offs, j):
        top, left = offs[0, 0, j, 0], offs[0, 0, j, 1]
        self.t0, self.l0 = lax.shift_right_logical(top, 8), lax.shift_right_logical(left, 8)
        self.tr, self.lr = top & (N - 1), left & (N - 1)
        self.t1, self.l1 = jnp.minimum(self.t0 + 1, 2), jnp.minimum(self.l0 + 1, 2)
        self.rows = lax.broadcasted_iota(jnp.int32, (N, N), 0) >= self.tr
        self.cols = lax.broadcasted_iota(jnp.int32, (N, N), 1) >= self.lr

    def take(self, blocks, plane):
        upper = jnp.where(self.cols, blocks[plane, self.t0, self.l0], blocks[plane, self.t0, self.l1])
        lower = jnp.where(self.cols, blocks[plane, self.t1, self.l0], blocks[plane, self.t1, self.l1])
        return jnp.where(self.rows, upper, lower)

    def add(self, blocks, plane, value):
        upper = jnp.where(self.rows, value, 0.0)
        lower = jnp.where(self.rows, 0.0, value)
        for t, part in ((self.t0, upper), (self.t1, lower)):
            blocks[plane, t, self.l0] += jnp.where(self.cols, part, 0.0)
            blocks[plane, t, self.l1] += jnp.where(self.cols, 0.0, part)

    def shifted(self, probe):
        return tuple(pltpu.roll(pltpu.roll(probe[p], self.tr, 0), self.lr, 1) for p in range(2))


def run_copies(pairs, sems):
    copies = [pltpu.make_async_copy(a, b, sems.at[i]) for i, (a, b) in enumerate(pairs)]
    for c in copies:
        c.start()
    for c in copies:
        c.wait()


N_IN = 34


def fill_padded(padded, sems, s, k, amp, ph, left, right, above, below, corner_a, corner_b):
    pairs = []
    for rb, ro, rs, rn in SEGMENTS:
        rd, rr = pl.ds(ro, rn), pl.ds(rs, rn)
        for cb, co, cs, cn in SEGMENTS:
            for p, source in enumerate((amp, ph)):
                pairs.append((source.at[s, rr, pl.ds(cs, cn)], padded.at[p, rb, cb, rd, pl.ds(co, cn)]))
        pairs.append((left.at[:, k, rr, :], padded.at[:, rb, 0, rd, pl.ds(0, H)]))
        pairs.append((right.at[:, k, rr, :], padded.at[:, rb, 2, rd, pl.ds(H, H)]))
        pairs.append((above.at[:, s, :, rr], padded.at[:, 0, rb, pl.ds(0, H), rd]))
        pairs.append((below.at[:, s, :, rr], padded.at[:, 2, rb, pl.ds(H, H), rd]))
    for source, rb, ro in ((corner_a, 0, 0), (corner_b, 2, H)):
        pairs.append((source.at[:, k, :, pl.ds(0, H)], padded.at[:, rb, 0, pl.ds(ro, H), pl.ds(0, H)]))
        pairs.append((source.at[:, k, :, pl.ds(H, H)], padded.at[:, rb, 2, pl.ds(ro, H), pl.ds(H, H)]))
    run_copies(pairs, sems)


N_OUT = 21


def drain_totals(totals, sems, centre, top, bottom, left, right):
    pairs = []
    for rb, ro, rs, rn in SEGMENTS:
        rd, rr = pl.ds(ro, rn), pl.ds(rs, rn)
        for cb, co, cs, cn in SEGMENTS:
            pairs.append((totals.at[:, rb, cb, rd, pl.ds(co, cn)], centre.at[:, rr, pl.ds(cs, cn)]))
        pairs.append((totals.at[:, rb, 0, rd, pl.ds(0, H)], left.at[:, rr, :]))
        pairs.append((totals.at[:, rb, 2, rd, pl.ds(H, H)], right.at[:, rr, :]))
        pairs.append((totals.at[:, 0, rb, pl.ds(0, H), :], top.at[:, :, pl.ds(rb * N, N)]))
        pairs.append((totals.at[:, 2, rb, pl.ds(H, H), :], bottom.at[:, :, pl.ds(rb * N, N)]))
    run_copies(pairs, sems)


def fold_shapes(planes):
    shape = lambda *s: jax.ShapeDtypeStruct((planes, *s), F32)
    return [shape(TILE, TILE), shape(H, 3 * N), shape(H, 3 * N), shape(TILE, H), shape(TILE, H)]


ANY = pl.BlockSpec(memory_space=pl.ANY)
SMEM = pl.BlockSpec(memory_space=pltpu.SMEM)
VMEM = pl.BlockSpec(memory_space=pltpu.VMEM)
PER_SLOT = pl.BlockSpec((1, 2, N, N), lambda j: (j, 0, 0, 0))
SLOT_SHAPE = jax.ShapeDtypeStruct((SLOTS, 2, N, N), F32)
PARAMS = pltpu.CompilerParams(dimension_semantics=("arbitrary",))


def window_of(padded, place):
    amp, ph = place.take(padded, 0), place.take(padded, 1)
    sine, cosine = sincos(ph)
    return amp * cosine, amp * sine


def intensity(wave):
    return wave[0] * wave[0] + wave[1] * wave[1]


def forward(s, k, scalars, halos, incident, prop, prop_t):
    lights = 2 if s == 0 else 1

    def kernel(offs, count, amp, ph, left, right, above, below, ca, cb, wave_ref, prop, prop_t, *rest):
        outs = list(rest)
        next_ref = outs.pop(0)
        window_ref = outs.pop(0) if s > 0 else None
        fold = outs[:5]
        padded, totals, sems = outs[5:]
        j = pl.program_id(0)

        @pl.when(j == 0)
        def _():
            totals[...] = jnp.zeros_like(totals)
            fill_padded(padded, sems, s, k, amp, ph, left, right, above, below, ca, cb)

        @pl.when(j < count[0, 0])
        def _():
            place = Place(offs, j)
            wave = place.shifted(wave_ref) if s == 0 else (wave_ref[0, 0], wave_ref[0, 1])
            window = window_of(padded, place)
            if s > 0:
                window_ref[0, 0], window_ref[0, 1] = window
            after = both_axes(product_of(wave, window), prop, prop_t, True, True)
            next_ref[0, 0], next_ref[0, 1] = after
            if s == 0:
                place.add(totals, 0, intensity(wave))
            place.add(totals, lights - 1, intensity(after))

        @pl.when(j == SLOTS - 1)
        def _():
            drain_totals(totals, sems, *fold)

    slot_outs = 1 if s == 0 else 2
    out = pl.pallas_call(
        kernel,
        name=f"forward_{s}",
        grid=(SLOTS,),
        in_specs=[SMEM, SMEM] + [ANY] * 8 + [VMEM if s == 0 else PER_SLOT, VMEM, VMEM],
        out_specs=[PER_SLOT] * slot_outs + [ANY] * 5,
        out_shape=[SLOT_SHAPE] * slot_outs + fold_shapes(lights),
        scratch_shapes=[
            pltpu.VMEM((2, 3, 3, N, N), F32),
            pltpu.VMEM((lights, 3, 3, N, N), F32),
            pltpu.SemaphoreType.DMA((N_IN,)),
        ],
        compiler_params=PARAMS,
    )(*scalars, *halos, incident, prop, prop_t)
    return out[0], (out[1] if s > 0 else None), out[slot_outs:]


def turn(s, k, scalars, halos, incident, target, prop, prop_t, dft, dft_t):
    def kernel(offs, count, amp, ph, left, right, above, below, ca, cb, wave_ref, target_ref, prop, prop_t, dft, dft_t,
               back_ref, centre, top, bottom, left_o, right_o, padded, totals, sems):
        j = pl.program_id(0)

        @pl.when(j == 0)
        def _():
            totals[...] = jnp.zeros_like(totals)
            fill_padded(padded, sems, s, k, amp, ph, left, right, above, below, ca, cb)

        @pl.when(j < count[0, 0])
        def _():
            place = Place(offs, j)
            wave = (wave_ref[0, 0], wave_ref[0, 1])
            window = window_of(padded, place)
            far = both_axes(product_of(wave, window), dft, dft_t, True, False)
            misfit = intensity(far) - target_ref[0]
            back = both_axes((misfit * far[0], misfit * far[1]), dft_t, dft, False, True)
            grad = conj_product(wave, back)
            place.add(totals, 0, grad[0])
            place.add(totals, 1, grad[1])
            back_ref[0, 0], back_ref[0, 1] = both_axes(conj_product(window, back), prop_t, prop, True, True)

        @pl.when(j == SLOTS - 1)
        def _():
            drain_totals(totals, sems, centre, top, bottom, left_o, right_o)

    out = pl.pallas_call(
        kernel,
        name=f"turn_{s}",
        grid=(SLOTS,),
        in_specs=[SMEM, SMEM] + [ANY] * 8 + [PER_SLOT, pl.BlockSpec((1, N, N), lambda j: (j, 0, 0))] + [VMEM] * 4,
        out_specs=[PER_SLOT] + [ANY] * 5,
        out_shape=[SLOT_SHAPE] + fold_shapes(2),
        scratch_shapes=[
            pltpu.VMEM((2, 3, 3, N, N), F32),
            pltpu.VMEM((2, 3, 3, N, N), F32),
            pltpu.SemaphoreType.DMA((N_IN,)),
        ],
        compiler_params=PARAMS,
    )(*scalars, *halos, incident, target, prop, prop_t, dft, dft_t)
    return out[0], out[1:]


def backward(s, scalars, incident, window, back, prop, prop_t):
    def kernel(offs, count, *rest):
        rest = list(rest)
        wave_ref = rest.pop(0)
        window_ref = rest.pop(0) if s > 0 else None
        back_ref = rest.pop(0)
        if s > 0:
            prop, prop_t = rest.pop(0), rest.pop(0)
            before_ref = rest.pop(0)
        fold, totals, sems = rest[:5], rest[5], rest[6]
        j = pl.program_id(0)

        @pl.when(j == 0)
        def _():
            totals[...] = jnp.zeros_like(totals)

        @pl.when(j < count[0, 0])
        def _():
            place = Place(offs, j)
            wave = place.shifted(wave_ref) if s == 0 else (wave_ref[0, 0], wave_ref[0, 1])
            back = (back_ref[0, 0], back_ref[0, 1])
            grad = conj_product(wave, back)
            place.add(totals, 0, grad[0])
            place.add(totals, 1, grad[1])
            if s > 0:
                window = (window_ref[0, 0], window_ref[0, 1])
                before_ref[0, 0], before_ref[0, 1] = both_axes(conj_product(window, back), prop_t, prop, True, True)

        @pl.when(j == SLOTS - 1)
        def _():
            drain_totals(totals, sems, *fold)

    operands = [incident, window, back, prop, prop_t] if s > 0 else [incident, back]
    specs = [PER_SLOT] * 3 + [VMEM] * 2 if s > 0 else [VMEM, PER_SLOT]
    slot_outs = 1 if s > 0 else 0
    out = pl.pallas_call(
        kernel,
        name=f"backward_{s}",
        grid=(SLOTS,),
        in_specs=[SMEM, SMEM] + specs,
        out_specs=[PER_SLOT] * slot_outs + [ANY] * 5,
        out_shape=[SLOT_SHAPE] * slot_outs + fold_shapes(2),
        scratch_shapes=[pltpu.VMEM((2, 3, 3, N, N), F32), pltpu.SemaphoreType.DMA((N_OUT,))],
        compiler_params=PARAMS,
    )(*scalars, *operands)
    return (out[0] if s > 0 else None), out[slot_outs:]


def reorder_targets(measured):
    def kernel(m_ref, o_ref):
        r = lax.broadcasted_iota(jnp.int32, (N, N), 0)
        c = lax.broadcasted_iota(jnp.int32, (N, N), 1)

        def one_hot(to, source):
            return jnp.where(source == jnp.where(to < H, 2 * to, 2 * to - (N - 1)), 1.0, 0.0).astype(BF16)

        def thirds(x):
            a = x.astype(BF16)
            rest = x - a.astype(F32)
            b = rest.astype(BF16)
            return a, b, (rest - b.astype(F32)).astype(BF16)

        rows, cols = one_hot(r, c), one_hot(c, r)
        a, b, d = thirds(m_ref[0, 0, 0])
        x = (dot(rows, a) + dot(rows, b)) + dot(rows, d)
        a, b, d = thirds(x)
        o_ref[0] = (dot(a, cols) + dot(b, cols)) + dot(d, cols)

    return pl.pallas_call(
        kernel,
        name="reorder",
        grid=(SLOTS,),
        in_specs=[pl.BlockSpec((1, 1, 1, N, N), lambda j: (0, 0, j, 0, 0))],
        out_specs=pl.BlockSpec((1, N, N), lambda j: (j, 0, 0)),
        out_shape=jax.ShapeDtypeStruct((SLOTS, N, N), F32),
        compiler_params=PARAMS,
    )(measured)


def rims_with_rows(left, right, from_above, from_below):
    planes = left.shape[0]

    def kernel(l_ref, r_ref, fa, fb, lo, ro):
        for source, out, c in ((l_ref, lo, 0), (r_ref, ro, 3 * N - H)):
            out[:, :H, :] = source[:, :H, :] + fa[:, :, c:c + H]
            out[:, H:TILE - H, :] = source[:, H:TILE - H, :]
            out[:, TILE - H:, :] = source[:, TILE - H:, :] + fb[:, :, c:c + H]

    return pl.pallas_call(
        kernel,
        name="rims",
        in_specs=[VMEM] * 4,
        out_specs=[VMEM] * 2,
        out_shape=[jax.ShapeDtypeStruct((planes, TILE, H), F32)] * 2,
    )(left, right, from_above, from_below)


def shifted(value, axis, steps):
    count = lax.axis_size(axis)
    leading, last = max(0, -steps), min(count, count - steps)
    return lax.ppermute(value, axis, [(source, source + steps) for source in range(leading, last)])


def fold(parts):
    centre, top, bottom, left, right = parts
    from_above = shifted(bottom, "row", 1)
    from_below = shifted(top, "row", -1)
    to_left, to_right = rims_with_rows(left, right, from_above, from_below)
    from_left = shifted(to_right, "col", 1)
    from_right = shifted(to_left, "col", -1)
    return centre, from_above, from_below, from_left, from_right


def update(s, amp, ph, grads, lights, plane, previous):
    strips = TILE // H

    def kernel(amp_ref, ph_ref, *rest):
        g, l = rest[:5], rest[5:10]
        out_r, out_i = rest[-2:]
        i = pl.program_id(0)
        first, last = jnp.where(i == 0, 1.0, 0.0), jnp.where(i == strips - 1, 1.0, 0.0)

        def total(refs, p):
            centre, above, below, left, right = refs
            x = centre[p] + jnp.where(i == 0, above[p, :, H:H + TILE], 0.0) + jnp.where(i == strips - 1, below[p, :, H:H + TILE], 0.0)
            return jnp.concatenate([x[:, :H] + left[p], x[:, H:TILE - H], x[:, TILE - H:] + right[p]], 1)

        scale = 1.0 / (total(l, 0) + 1.0)
        sine, cosine = sincos(ph_ref[0])
        out_r[0] = amp_ref[0] * cosine - total(g, 0) * scale
        out_i[0] = amp_ref[0] * sine - total(g, 1) * scale

    def specs(planes, at):
        strip = lambda cols: pl.BlockSpec((planes, H, cols), lambda i: (at, i, 0))
        whole = pl.BlockSpec((planes, H, 3 * N), lambda i: (at, 0, 0))
        return [strip(TILE), whole, whole, strip(H), strip(H)]

    one = pl.BlockSpec((1, H, TILE), lambda i: (s, i, 0))
    shape = jax.ShapeDtypeStruct((SLICES, TILE, TILE), F32)
    previous = list(previous or [])
    return pl.pallas_call(
        kernel,
        name=f"update_{s}",
        grid=(strips,),
        in_specs=[one, one] + specs(2, 0) + specs(1, plane) + [ANY] * len(previous),
        out_specs=[one, one],
        out_shape=[shape, shape],
        input_output_aliases={12: 0, 13: 1} if previous else {},
        compiler_params=PARAMS,
    )(amp, ph, *grads, *lights, *previous)


def body(object_amp, object_phase, probe_field, measured, offsets, counts):
    prop, prop_t, dft, dft_t = (jnp.asarray(t) for t in tables())
    amp, ph = object_amp, object_phase
    scalars = (offsets, counts)
    sides = []
    for chunk in CHUNKS:
        a, b = chunk[0], chunk[-1] + 1
        edge = lambda cols: jnp.stack([amp[a:b, :, cols], ph[a:b, :, cols]])
        left = shifted(edge(slice(TILE - H, TILE)), "col", 1)
        right = shifted(edge(slice(0, H)), "col", -1)
        sides.append((left, right))
    above = shifted(jnp.stack([amp[:, TILE - H:], ph[:, TILE - H:]]), "row", 1)
    below = shifted(jnp.stack([amp[:, :H], ph[:, :H]]), "row", -1)
    halos = {}
    for chunk, (left, right) in zip(CHUNKS, sides):
        corner = lambda rows: jnp.concatenate([left[:, :, rows], right[:, :, rows]], 3)
        corner_a = shifted(corner(slice(TILE - H, TILE)), "row", 1)
        corner_b = shifted(corner(slice(0, H)), "row", -1)
        for k, s in enumerate(chunk):
            halos[s] = (k, (amp, ph, left, right, above, below, corner_a, corner_b))
    target = reorder_targets(measured)

    incident, windows, lights = [probe_field], [None], []
    for s in range(SLICES - 1):
        k, arrays = halos[s]
        wave, window, light = forward(s, k, scalars, arrays, incident[s], prop, prop_t)
        incident.append(wave)
        windows.append(window)
        lights.append(fold(light))
    k, arrays = halos[SLICES - 1]
    back, grad = turn(SLICES - 1, k, scalars, arrays, incident[-1], target, prop, prop_t, dft, dft_t)
    light_of = {0: (lights[0], 0), 1: (lights[0], 1), 2: (lights[1], 0), 3: (lights[2], 0)}
    outs = None
    for s in reversed(range(SLICES)):
        if s < SLICES - 1:
            back, grad = backward(s, scalars, incident[s], windows[s + 1], back, prop, prop_t)
        outs = update(s, amp, ph, fold(grad), *light_of[s], outs)
    return tuple(outs)


def solution(mesh):
    placed = (
        P(None, "row", "col"),
        P(None, "row", "col"),
        P(),
        P("row", "col", None, None, None),
        P("row", "col", None, None),
        P("row", "col"),
    )
    return jax.shard_map(
        body,
        mesh=mesh,
        in_specs=placed,
        out_specs=(P(None, "row", "col"), P(None, "row", "col")),
        check_vma=False,
    )
```

```python
import jax
import jax.numpy as jnp
import numpy as np
from jax import lax
from jax.experimental import pallas as pl
from jax.experimental.pallas import tpu as pltpu
from jax.sharding import PartitionSpec as P


FRESNEL = 0.0005
N = 256
H = 128
SLICES = 4
SLOTS = 4
TILE = 512
F32 = jnp.float32
BF16 = jnp.bfloat16

SEGMENTS = ((0, H, 0, H), (1, 0, H, N), (2, 0, H + N, H))


def real_form(matrix):
    return np.block([[matrix.real, -matrix.imag], [matrix.imag, matrix.real]])


def split_table(pair):
    parts = np.stack([real_form(m) for m in pair]).astype(np.float32)
    high = parts.astype(BF16)
    low = (parts - high.astype(np.float32)).astype(BF16)
    return np.stack([high, low])


def tables():
    counter = np.arange(N)
    frequency = (counter + H) % N - H
    q = np.exp(1j * FRESNEL * frequency.astype(np.float64) ** 2)
    spread = np.fft.ifft(q)
    j, m = np.arange(H)[:, None], np.arange(H)[None, :]
    near, far = spread[(j - m) % N], spread[(j - m - H) % N]
    prop = ((near + far) / 2, (near - far) / 2)
    even = np.exp(-2j * np.pi * ((j * m) % H) / H) / 16
    odd = np.exp(-2j * np.pi * ((m * (2 * j + 1)) % N) / N) / 16
    prop_table, dft_table = split_table(prop), split_table((even, odd))
    return prop_table, dft_table


def fit_sincos():
    u = np.cos(np.linspace(0, np.pi, 4001)) * 0.79
    w = u * u
    sin_part = np.polynomial.polynomial.polyfit(w, np.where(u == 0, 1.0, np.sin(u) / np.where(u == 0, 1.0, u)), 4)
    cos_part = np.polynomial.polynomial.polyfit(w, np.cos(u), 4)
    return [float(c) for c in sin_part], [float(c) for c in cos_part]


SIN_PART, COS_PART = fit_sincos()


def poly(w, coefficients):
    total = jnp.full_like(w, coefficients[-1])
    for c in coefficients[-2::-1]:
        total = total * w + c
    return total


def sincos(phase):
    u = phase * 0.25
    w = u * u
    s, c = u * poly(w, SIN_PART), poly(w, COS_PART)
    s, c = 2.0 * s * c, 1.0 - 2.0 * s * s
    return 2.0 * s * c, 1.0 - 2.0 * s * s


def split(x):
    high = x.astype(BF16)
    return high, (x - high.astype(F32)).astype(BF16)


def dot(a, b):
    return jnp.dot(a, b, preferred_element_type=F32)


def left_product(table, which, z):
    zh, zl = split(z)
    mh, ml = table[0, which], table[1, which]
    return dot(mh, zh) + dot(ml, zh) + dot(mh, zl)


def right_product(table, which, z):
    zh, zl = split(z)
    mh, ml = table[0, which], table[1, which]
    return dot(zh, mh) + dot(zh, ml) + dot(zl, mh)


def halves(x, axis):
    return (x[:H], x[H:]) if axis == 0 else (x[:, :H], x[:, H:])


def along(wave, axis, table, before, after):
    (r0, r1), (i0, i1) = halves(wave[0], axis), halves(wave[1], axis)
    if before:
        r0, r1, i0, i1 = r0 + r1, r0 - r1, i0 + i1, i0 - i1
    product = left_product if axis == 0 else right_product
    first = product(table, 0, jnp.concatenate([r0, i0], axis))
    second = product(table, 1, jnp.concatenate([r1, i1], axis))
    (r0, i0), (r1, i1) = halves(first, axis), halves(second, axis)
    if after:
        r0, r1, i0, i1 = r0 + r1, r0 - r1, i0 + i1, i0 - i1
    return jnp.concatenate([r0, r1], axis), jnp.concatenate([i0, i1], axis)


def both_axes(wave, left, right, before, after):
    wave = along(wave, 0, left, before, after)
    return along(wave, 1, right, before, after)


def product_of(a, b):
    return a[0] * b[0] - a[1] * b[1], a[0] * b[1] + a[1] * b[0]


def conj_product(a, b):
    return a[0] * b[0] + a[1] * b[1], a[0] * b[1] - a[1] * b[0]


class Place:
    def __init__(self, offs, j):
        top, left = offs[0, 0, j, 0], offs[0, 0, j, 1]
        self.t0, self.l0 = lax.shift_right_logical(top, 8), lax.shift_right_logical(left, 8)
        self.tr, self.lr = top & (N - 1), left & (N - 1)
        self.t1, self.l1 = jnp.minimum(self.t0 + 1, 2), jnp.minimum(self.l0 + 1, 2)
        self.rows = lax.broadcasted_iota(jnp.int32, (N, N), 0) >= self.tr
        self.cols = lax.broadcasted_iota(jnp.int32, (N, N), 1) >= self.lr

    def take(self, blocks, plane):
        upper = jnp.where(self.cols, blocks[plane, self.t0, self.l0], blocks[plane, self.t0, self.l1])
        lower = jnp.where(self.cols, blocks[plane, self.t1, self.l0], blocks[plane, self.t1, self.l1])
        return jnp.where(self.rows, upper, lower)

    def add(self, blocks, plane, value):
        upper = jnp.where(self.rows, value, 0.0)
        lower = jnp.where(self.rows, 0.0, value)
        for t, part in ((self.t0, upper), (self.t1, lower)):
            blocks[plane, t, self.l0] += jnp.where(self.cols, part, 0.0)
            blocks[plane, t, self.l1] += jnp.where(self.cols, 0.0, part)

    def shifted(self, probe):
        return tuple(pltpu.roll(pltpu.roll(probe[p], self.tr, 0), self.lr, 1) for p in range(2))


N_IN = 34


def fill_pairs(padded, s, k, amp, ph, left, right, above, below, corner_a, corner_b):
    pairs = []
    for rb, ro, rs, rn in SEGMENTS:
        rd, rr = pl.ds(ro, rn), pl.ds(rs, rn)
        for cb, co, cs, cn in SEGMENTS:
            for p, source in enumerate((amp, ph)):
                pairs.append((source.at[s, rr, pl.ds(cs, cn)], padded.at[p, rb, cb, rd, pl.ds(co, cn)]))
        pairs.append((left.at[:, k, rr, :], padded.at[:, rb, 0, rd, pl.ds(0, H)]))
        pairs.append((right.at[:, k, rr, :], padded.at[:, rb, 2, rd, pl.ds(H, H)]))
        pairs.append((above.at[:, s, :, rr], padded.at[:, 0, rb, pl.ds(0, H), rd]))
        pairs.append((below.at[:, s, :, rr], padded.at[:, 2, rb, pl.ds(H, H), rd]))
    for source, rb, ro in ((corner_a, 0, 0), (corner_b, 2, H)):
        pairs.append((source.at[:, k, :, pl.ds(0, H)], padded.at[:, rb, 0, pl.ds(ro, H), pl.ds(0, H)]))
        pairs.append((source.at[:, k, :, pl.ds(H, H)], padded.at[:, rb, 2, pl.ds(ro, H), pl.ds(H, H)]))
    return pairs


def copies_of(pairs, sems):
    return [pltpu.make_async_copy(a, b, sems.at[i]) for i, (a, b) in enumerate(pairs)]


def start_all(copies):
    for c in copies:
        c.start()


def wait_all(copies):
    for c in copies:
        c.wait()


def drain_pairs(totals, first, planes, by_columns, centre, top, bottom, left, right):
    own, pairs = pl.ds(first, planes), []
    for rb, ro, rs, rn in SEGMENTS:
        rd, rr = pl.ds(ro, rn), pl.ds(rs, rn)
        for cb, co, cs, cn in SEGMENTS:
            pairs.append((totals.at[own, rb, cb, rd, pl.ds(co, cn)], centre.at[:, rr, pl.ds(cs, cn)]))
        whole = pl.ds(rb * N, N)
        if by_columns:
            pairs.append((totals.at[own, rb, 0, :, pl.ds(0, H)], left.at[:, whole, :]))
            pairs.append((totals.at[own, rb, 2, :, pl.ds(H, H)], right.at[:, whole, :]))
            pairs.append((totals.at[own, 0, rb, pl.ds(0, H), rd], top.at[:, :, rr]))
            pairs.append((totals.at[own, 2, rb, pl.ds(H, H), rd], bottom.at[:, :, rr]))
        else:
            pairs.append((totals.at[own, rb, 0, rd, pl.ds(0, H)], left.at[:, rr, :]))
            pairs.append((totals.at[own, rb, 2, rd, pl.ds(H, H)], right.at[:, rr, :]))
            pairs.append((totals.at[own, 0, rb, pl.ds(0, H), :], top.at[:, :, whole]))
            pairs.append((totals.at[own, 2, rb, pl.ds(H, H), :], bottom.at[:, :, whole]))
    return pairs


def fold_shapes(planes, by_columns=False):
    shape = lambda *s: jax.ShapeDtypeStruct((planes, *s), F32)
    wide, tall = (TILE, 3 * N) if by_columns else (3 * N, TILE)
    return [shape(TILE, TILE), shape(H, wide), shape(H, wide), shape(tall, H), shape(tall, H)]


ANY = pl.BlockSpec(memory_space=pl.ANY)
SMEM = pl.BlockSpec(memory_space=pltpu.SMEM)
VMEM = pl.BlockSpec(memory_space=pltpu.VMEM)
PER_SLOT = pl.BlockSpec((1, 2, N, N), lambda j: (j, 0, 0, 0))
SLOT_SHAPE = jax.ShapeDtypeStruct((SLOTS, 2, N, N), F32)
PARAMS = pltpu.CompilerParams(dimension_semantics=("arbitrary",))
BLOCKS = lambda planes: pltpu.VMEM((planes, 3, 3, N, N), F32)


def window_of(padded, place):
    amp, ph = place.take(padded, 0), place.take(padded, 1)
    sine, cosine = sincos(ph)
    return amp * cosine, amp * sine


def intensity(wave):
    return wave[0] * wave[0] + wave[1] * wave[1]


def wave_in(ref):
    return ref[0, 0], ref[0, 1]


def put_wave(ref, wave):
    ref[0, 0], ref[0, 1] = wave


def enter(scalars, sides, probe, prop, prop_t):
    def kernel(offs, count, *rest):
        arrays, (probe, prop, prop_t) = rest[:8], rest[8:11]
        waves, window_ref, parts = rest[11:14], rest[14], rest[15:20]
        padded, totals, sems = rest[20:]
        j = pl.program_id(0)
        fills = [copies_of(fill_pairs(padded.at[s], s, s, *arrays), sems.at[s]) for s in range(2)]

        @pl.when(j == 0)
        def _():
            start_all(fills[0])
            start_all(fills[1])
            totals[...] = jnp.zeros_like(totals)
            wait_all(fills[0])

        @pl.when(j < count[0, 0])
        def _():
            place = Place(offs, j)
            wave = place.shifted(probe)
            put_wave(waves[0], wave)
            place.add(totals, 0, intensity(wave))
            wave = both_axes(product_of(wave, window_of(padded.at[0], place)), prop, prop_t, True, True)
            put_wave(waves[1], wave)
            place.add(totals, 1, intensity(wave))

        @pl.when(j == 0)
        def _():
            wait_all(fills[1])

        @pl.when(j < count[0, 0])
        def _():
            place = Place(offs, j)
            window = window_of(padded.at[1], place)
            put_wave(window_ref, window)
            wave = both_axes(product_of(wave_in(waves[1]), window), prop, prop_t, True, True)
            put_wave(waves[2], wave)
            place.add(totals, 2, intensity(wave))

        @pl.when(j == SLOTS - 1)
        def _():
            drains = copies_of(drain_pairs(totals, 0, 3, True, *parts), sems.at[0])
            start_all(drains)
            wait_all(drains)

    out = pl.pallas_call(
        kernel,
        name="enter",
        grid=(SLOTS,),
        in_specs=[SMEM, SMEM] + [ANY] * 8 + [VMEM] * 3,
        out_specs=[PER_SLOT] * 4 + [ANY] * 5,
        out_shape=[SLOT_SHAPE] * 4 + fold_shapes(3, True),
        scratch_shapes=[pltpu.VMEM((2, 2, 3, 3, N, N), F32), BLOCKS(3), pltpu.SemaphoreType.DMA((2, N_IN))],
        compiler_params=PARAMS,
    )(*scalars, *sides, probe, prop, prop_t)
    return out[:3], out[3], out[4:]


def turn(scalars, sides, incident, target, prop, prop_t, dft, dft_t):
    def kernel(offs, count, *rest):
        arrays, (wave_ref, target_ref, prop, prop_t, dft, dft_t) = rest[:8], rest[8:14]
        back_ref, parts = rest[14], rest[15:20]
        padded, totals, kept, sems = rest[20:]
        j = pl.program_id(0)
        fills = [copies_of(fill_pairs(padded.at[k], k + 2, k, *arrays), sems.at[k]) for k in range(2)]

        @pl.when(j == 0)
        def _():
            start_all(fills[0])
            start_all(fills[1])
            totals[...] = jnp.zeros_like(totals)
            wait_all(fills[0])

        @pl.when(j < count[0, 0])
        def _():
            place = Place(offs, j)
            window = window_of(padded.at[0], place)
            kept[0, 0], kept[0, 1] = window
            wave = both_axes(product_of(wave_in(wave_ref), window), prop, prop_t, True, True)
            kept[1, 0], kept[1, 1] = wave
            place.add(totals, 4, intensity(wave))

        @pl.when(j == 0)
        def _():
            wait_all(fills[1])

        @pl.when(j < count[0, 0])
        def _():
            place = Place(offs, j)
            window = window_of(padded.at[1], place)
            wave = (kept[1, 0], kept[1, 1])
            far = both_axes(product_of(wave, window), dft, dft_t, True, False)
            misfit = intensity(far) - target_ref[0]
            back = both_axes((misfit * far[0], misfit * far[1]), dft_t, dft, False, True)
            grad = conj_product(wave, back)
            place.add(totals, 0, grad[0])
            place.add(totals, 1, grad[1])
            back = both_axes(conj_product(window, back), prop_t, prop, True, True)
            grad = conj_product(wave_in(wave_ref), back)
            place.add(totals, 2, grad[0])
            place.add(totals, 3, grad[1])
            back = both_axes(conj_product((kept[0, 0], kept[0, 1]), back), prop_t, prop, True, True)
            put_wave(back_ref, back)

        @pl.when(j == SLOTS - 1)
        def _():
            drains = copies_of(drain_pairs(totals, 0, 5, False, *parts), sems.at[0])
            start_all(drains)
            wait_all(drains)

    out = pl.pallas_call(
        kernel,
        name="turn",
        grid=(SLOTS,),
        in_specs=[SMEM, SMEM] + [ANY] * 8 + [PER_SLOT, pl.BlockSpec((1, N, N), lambda j: (j, 0, 0))] + [VMEM] * 4,
        out_specs=[PER_SLOT] + [ANY] * 5,
        out_shape=[SLOT_SHAPE] + fold_shapes(5),
        scratch_shapes=[
            pltpu.VMEM((2, 2, 3, 3, N, N), F32),
            BLOCKS(5),
            pltpu.VMEM((2, 2, N, N), F32),
            pltpu.SemaphoreType.DMA((2, N_IN)),
        ],
        compiler_params=PARAMS,
    )(*scalars, *sides, incident, target, prop, prop_t, dft, dft_t)
    return out[0], out[1:]


def leave(scalars, incident_0, incident_1, window_1, back, prop, prop_t):
    def kernel(offs, count, wave_0, wave_1, window_ref, back_ref, prop, prop_t, *rest):
        parts, (totals, sems) = rest[:5], rest[5:]
        j = pl.program_id(0)

        @pl.when(j == 0)
        def _():
            totals[...] = jnp.zeros_like(totals)

        @pl.when(j < count[0, 0])
        def _():
            place = Place(offs, j)
            back = wave_in(back_ref)
            grad = conj_product(wave_in(wave_1), back)
            place.add(totals, 0, grad[0])
            place.add(totals, 1, grad[1])
            back = both_axes(conj_product(wave_in(window_ref), back), prop_t, prop, True, True)
            grad = conj_product(wave_in(wave_0), back)
            place.add(totals, 2, grad[0])
            place.add(totals, 3, grad[1])

        @pl.when(j == SLOTS - 1)
        def _():
            drains = copies_of(drain_pairs(totals, 0, 4, False, *parts), sems)
            start_all(drains)
            wait_all(drains)

    return pl.pallas_call(
        kernel,
        name="leave",
        grid=(SLOTS,),
        in_specs=[SMEM, SMEM] + [PER_SLOT] * 4 + [VMEM] * 2,
        out_specs=[ANY] * 5,
        out_shape=fold_shapes(4),
        scratch_shapes=[BLOCKS(4), pltpu.SemaphoreType.DMA((N_IN,))],
        compiler_params=PARAMS,
    )(*scalars, incident_0, incident_1, window_1, back, prop, prop_t)


def reorder_targets(measured):
    def kernel(m_ref, o_ref):
        r = lax.broadcasted_iota(jnp.int32, (N, N), 0)
        c = lax.broadcasted_iota(jnp.int32, (N, N), 1)

        def one_hot(to, source):
            return jnp.where(source == jnp.where(to < H, 2 * to, 2 * to - (N - 1)), 1.0, 0.0).astype(BF16)

        def thirds(x):
            a = x.astype(BF16)
            rest = x - a.astype(F32)
            b = rest.astype(BF16)
            return a, b, (rest - b.astype(F32)).astype(BF16)

        rows, cols = one_hot(r, c), one_hot(c, r)
        a, b, d = thirds(m_ref[0, 0, 0])
        x = (dot(rows, a) + dot(rows, b)) + dot(rows, d)
        a, b, d = thirds(x)
        o_ref[0] = (dot(a, cols) + dot(b, cols)) + dot(d, cols)

    return pl.pallas_call(
        kernel,
        name="reorder",
        grid=(SLOTS,),
        in_specs=[pl.BlockSpec((1, 1, 1, N, N), lambda j: (0, 0, j, 0, 0))],
        out_specs=pl.BlockSpec((1, N, N), lambda j: (j, 0, 0)),
        out_shape=jax.ShapeDtypeStruct((SLOTS, N, N), F32),
        compiler_params=PARAMS,
    )(measured)


def rims_with_rows(parts, from_above, from_below):
    left, right = parts[3:]
    planes = left.shape[0]

    def kernel(l_ref, r_ref, fal, far, fbl, fbr, lo, ro):
        for source, out, fa, fb in ((l_ref, lo, fal, fbl), (r_ref, ro, far, fbr)):
            out[:, :H, :] = source[:, :H, :] + fa[...]
            out[:, H:TILE - H, :] = source[:, H:TILE - H, :]
            out[:, TILE - H:, :] = source[:, TILE - H:, :] + fb[...]

    whole = pl.BlockSpec((planes, TILE, H), lambda i: (0, 0, 0))
    ends = [pl.BlockSpec((planes, H, H), lambda i: (0, 0, 0)), pl.BlockSpec((planes, H, H), lambda i: (0, 0, 5))]
    return pl.pallas_call(
        kernel,
        grid=(1,),
        in_specs=[whole] * 2 + ends * 2,
        out_specs=[whole] * 2,
        out_shape=[jax.ShapeDtypeStruct((planes, TILE, H), F32)] * 2,
    )(left, right, from_above, from_above, from_below, from_below)


def rims_with_columns(parts, from_left, from_right):
    top, bottom = parts[1:3]
    planes = top.shape[0]

    def kernel(t_ref, b_ref, flt, flb, frt, frb, to, bo):
        for source, out, fl, fr in ((t_ref, to, flt, frt), (b_ref, bo, flb, frb)):
            out[:, :, :H] = source[:, :, :H] + fl[...]
            out[:, :, H:TILE - H] = source[:, :, H:TILE - H]
            out[:, :, TILE - H:] = source[:, :, TILE - H:] + fr[...]

    whole = pl.BlockSpec((planes, H, TILE), lambda i: (0, 0, 0))
    ends = [pl.BlockSpec((planes, H, H), lambda i: (0, 0, 0)), pl.BlockSpec((planes, H, H), lambda i: (0, 5, 0))]
    return pl.pallas_call(
        kernel,
        name="light_rims",
        grid=(1,),
        in_specs=[whole] * 2 + ends * 2,
        out_specs=[whole] * 2,
        out_shape=[jax.ShapeDtypeStruct((planes, H, TILE), F32)] * 2,
    )(top, bottom, from_left, from_left, from_right, from_right)


def shifted(value, axis, steps):
    count = lax.axis_size(axis)
    leading, last = max(0, -steps), min(count, count - steps)
    return lax.ppermute(value, axis, [(source, source + steps) for source in range(leading, last)])


def light_scale(centre, from_left, from_right, from_above, from_below):
    planes, blocks = centre.shape[0], TILE // H

    def kernel(centre, left, right, above, below, out):
        c = pl.program_id(0)
        out[...] = centre[...]
        out[:, :H, :] += above[...]
        out[:, TILE - H:, :] += below[...]

        @pl.when(c == 0)
        def _():
            out[...] += left[:, H:H + TILE, :]

        @pl.when(c == blocks - 1)
        def _():
            out[...] += right[:, H:H + TILE, :]

        out[...] = 1.0 / (out[...] + 1.0)

    column = pl.BlockSpec((planes, TILE, H), lambda c: (0, 0, c))
    side = pl.BlockSpec((planes, 3 * N, H), lambda c: (0, 0, 0))
    end = pl.BlockSpec((planes, H, H), lambda c: (0, 0, c))
    return pl.pallas_call(
        kernel,
        name="light_scale",
        grid=(blocks,),
        in_specs=[column, side, side, end, end],
        out_specs=column,
        out_shape=jax.ShapeDtypeStruct((planes, TILE, TILE), F32),
        compiler_params=PARAMS,
    )(centre, from_left, from_right, from_above, from_below)


def update(slices, columns, amp, ph, centre, above, below, sides, scale, light_plane, previous, pair=0):
    base, stride = columns[0], (columns[1] - columns[0])
    touches = {0, 3} & set(columns)
    top_slice = slices[0]
    operands = [amp, ph, centre, above, below]
    column = lambda n, at: pl.BlockSpec((n, TILE, H), at)
    end = lambda n, at: pl.BlockSpec((n, H, H), at)
    of = lambda i: base + stride * i
    here = column(1, lambda a, i: (top_slice - a, 0, of(i)))
    specs = [here, here, column(2, lambda a, i: (a + pair, 0, of(i)))]
    specs += [end(2, lambda a, i: (a + pair, 0, of(i) + 1))] * 2
    if touches:
        operands += list(sides)
        specs += [column(2, lambda a, i: (a + pair, 0, 0))] * 2
    if light_plane is None:
        operands.append(scale)
        specs.append(column(1, lambda a, i: (top_slice - a, 0, of(i))))
    else:
        p = light_plane
        operands += [centre, above, below]
        specs += [column(1, lambda a, i: (p, 0, of(i)))] + [end(1, lambda a, i: (p, 0, of(i) + 1))] * 2
        if touches:
            operands += list(sides)
            specs += [column(1, lambda a, i: (p, 0, 0))] * 2
    used = len(operands)
    if previous:
        operands += list(previous)
        specs += [ANY] * 2

    def kernel(*refs):
        refs = list(refs)
        take = lambda: refs.pop(0)
        amp_ref, ph_ref = take(), take()
        c = of(pl.program_id(1))

        def total(p, parts):
            x = parts[0][p]
            x = jnp.concatenate([x[:H] + parts[1][p], x[H:TILE - H], x[TILE - H:] + parts[2][p]], 0)
            return x + side_of(c, parts[3][p], parts[4][p]) if touches else x

        grads = [take() for _ in range(5 if touches else 3)]
        if light_plane is None:
            scale = take()[0]
        else:
            scale = 1.0 / (total(0, [take() for _ in range(5 if touches else 3)]) + 1.0)
        out_r, out_i = refs[-2:]
        sine, cosine = sincos(ph_ref[0])
        out_r[0] = amp_ref[0] * cosine - total(0, grads) * scale
        out_i[0] = amp_ref[0] * sine - total(1, grads) * scale

    shape = jax.ShapeDtypeStruct((SLICES, TILE, TILE), F32)
    return pl.pallas_call(
        kernel,
        grid=(len(slices), len(columns)),
        in_specs=specs,
        out_specs=[here, here],
        out_shape=[shape, shape],
        input_output_aliases={used: 0, used + 1: 1} if previous else {},
        compiler_params=pltpu.CompilerParams(dimension_semantics=("arbitrary", "arbitrary")),
    )(*operands)


def side_of(c, left, right):
    return jnp.where(c == 0, left, jnp.where(c == TILE // H - 1, right, 0.0))


def program(object_amp, object_phase, probe_field, measured, offsets, counts):
    prop, dft = lax.optimization_barrier(tuple(jnp.asarray(t) for t in tables()))
    prop_t, dft_t = jnp.swapaxes(prop, 2, 3), jnp.swapaxes(dft, 2, 3)
    amp, ph = object_amp, object_phase
    scalars = (offsets, counts)
    edges = []
    for a, b in ((0, 2), (2, 4)):
        edge = lambda cols: jnp.stack([amp[a:b, :, cols], ph[a:b, :, cols]])
        left = shifted(edge(slice(TILE - H, TILE)), "col", 1)
        right = shifted(edge(slice(0, H)), "col", -1)
        edges.append((left, right))
    above = shifted(jnp.stack([amp[:, TILE - H:], ph[:, TILE - H:]]), "row", 1)
    below = shifted(jnp.stack([amp[:, :H], ph[:, :H]]), "row", -1)
    sides = []
    for left, right in edges:
        corner = lambda rows: jnp.concatenate([left[:, :, rows], right[:, :, rows]], 3)
        corner_a = shifted(corner(slice(TILE - H, TILE)), "row", 1)
        corner_b = shifted(corner(slice(0, H)), "row", -1)
        sides.append((amp, ph, left, right, above, below, corner_a, corner_b))
    target = reorder_targets(measured)

    waves, window_1, lights = enter(scalars, sides[0], probe_field, prop, prop_t)
    light_left = shifted(lights[4], "col", 1)
    light_right = shifted(lights[3], "col", -1)

    back, grads_a = turn(scalars, sides[1], waves[2], target, prop, prop_t, dft, dft_t)
    a_above = shifted(grads_a[2], "row", 1)
    a_below = shifted(grads_a[1], "row", -1)

    grads_b = leave(scalars, waves[0], waves[1], window_1, back, prop, prop_t)
    b_above = shifted(grads_b[2], "row", 1)
    b_below = shifted(grads_b[1], "row", -1)

    to_up, to_down = rims_with_columns(lights, light_left, light_right)
    light_above = shifted(to_down, "row", 1)
    light_below = shifted(to_up, "row", -1)

    to_left, to_right = rims_with_rows(grads_a, a_above, a_below)
    a_sides = shifted(to_right, "col", 1), shifted(to_left, "col", -1)
    scale = light_scale(lights[0], light_left, light_right, light_above, light_below)

    to_left, to_right = rims_with_rows(grads_b, b_above, b_below)
    b_sides = shifted(to_right, "col", 1), shifted(to_left, "col", -1)

    every, middle, ends = (0, 1, 2, 3), (1, 2), (0, 3)
    a_parts, b_parts = (grads_a[0], a_above, a_below), (grads_b[0], b_above, b_below)
    outs = update((1, 0), middle, amp, ph, *b_parts, None, scale, None, None)
    outs = update((3,), every, amp, ph, *a_parts, a_sides, None, 4, outs)
    outs = update((2,), every, amp, ph, *a_parts, a_sides, scale, None, outs, pair=1)
    outs = update((1, 0), ends, amp, ph, *b_parts, b_sides, scale, None, outs)
    return tuple(outs)


def solution(mesh):
    placed = (
        P(None, "row", "col"),
        P(None, "row", "col"),
        P(),
        P("row", "col", None, None, None),
        P("row", "col", None, None),
        P("row", "col"),
    )
    return jax.shard_map(
        program,
        mesh=mesh,
        in_specs=placed,
        out_specs=(P(None, "row", "col"), P(None, "row", "col")),
        check_vma=False,
    )
```

```python
import math

import jax
import jax.numpy as jnp
import numpy as np
from jax import lax
from jax.experimental import pallas as pl
from jax.experimental.pallas import tpu as pltpu
from jax.sharding import PartitionSpec as P


FRESNEL = 0.0005
N = 256
H = 128
SLICES = 4
SLOTS = 4
TILE = 512
F32 = jnp.float32
BF16 = jnp.bfloat16

G = 1
STEPS = SLOTS // G


def real_form(matrix):
    return np.block([[matrix.real, -matrix.imag], [matrix.imag, matrix.real]])


def split_table(pair):
    parts = np.stack([real_form(m) for m in pair]).astype(np.float32)
    high = parts.astype(BF16)
    low = (parts - high.astype(np.float32)).astype(BF16)
    return np.stack([high, low])


def tables():
    counter = np.arange(N)
    frequency = (counter + H) % N - H
    q = np.exp(1j * FRESNEL * frequency.astype(np.float64) ** 2)
    spread = np.fft.ifft(q)
    j, m = np.arange(H)[:, None], np.arange(H)[None, :]
    near, far = spread[(j - m) % N], spread[(j - m - H) % N]
    prop = ((near + far) / 2, (near - far) / 2)
    even = np.exp(-2j * np.pi * ((j * m) % H) / H) / 16
    odd = np.exp(-2j * np.pi * ((m * (2 * j + 1)) % N) / N) / 16
    prop_table, dft_table = split_table(prop), split_table((even, odd))
    return prop_table, dft_table


def fit_sincos():
    x = np.cos(np.linspace(0, np.pi, 4000)) * 3.16
    w = x * x
    fit = lambda y: [float(c) for c in np.polynomial.chebyshev.Chebyshev.fit(w, y, 3).convert(kind=np.polynomial.Polynomial).coef]
    return fit(np.sqrt(2.0) * np.sin(x / 4) / x), fit(2.0 * np.cos(x / 4))


SIN_PART, COS_PART = fit_sincos()
ROOT_2 = math.sqrt(2.0)


def poly(w, coefficients):
    total = coefficients[-1] * w + coefficients[-2]
    for c in coefficients[-3::-1]:
        total = total * w + c
    return total


def sincos(phase):
    w = phase * phase
    s, c = phase * poly(w, SIN_PART), poly(w, COS_PART)
    s2, c2 = s * c, 1.0 - s * s
    return ROOT_2 * (s2 * c2), 1.0 - s2 * s2


def split(x):
    high = x.astype(BF16)
    return high, (x - high.astype(F32)).astype(BF16)


def dot(a, b):
    return jnp.dot(a, b, preferred_element_type=F32)


def left_product(table, which, z):
    zh, zl = split(z)
    mh, ml = table[0, which], table[1, which]
    return dot(mh, zh) + dot(ml, zh) + dot(mh, zl)


def right_product(table, which, z):
    zh, zl = split(z)
    mh, ml = table[0, which], table[1, which]
    return dot(zh, mh) + dot(zh, ml) + dot(zl, mh)


def halves(x, axis):
    return (x[:H], x[H:]) if axis == 0 else (x[:, :H], x[:, H:])


def along(waves, axis, table, before, after):
    product = left_product if axis == 0 else right_product
    stacks = []
    for wave in waves:
        (r0, r1), (i0, i1) = halves(wave[0], axis), halves(wave[1], axis)
        if before:
            r0, r1, i0, i1 = r0 + r1, r0 - r1, i0 + i1, i0 - i1
        stacks.append((jnp.concatenate([r0, i0], axis), jnp.concatenate([r1, i1], axis)))
    stacks = [(product(table, 0, first), product(table, 1, second)) for first, second in stacks]
    outs = []
    for first, second in stacks:
        (r0, i0), (r1, i1) = halves(first, axis), halves(second, axis)
        if after:
            r0, r1, i0, i1 = r0 + r1, r0 - r1, i0 + i1, i0 - i1
        outs.append((jnp.concatenate([r0, r1], axis), jnp.concatenate([i0, i1], axis)))
    return outs


def both_axes(waves, left, right, before, after):
    return along(along(waves, 0, left, before, after), 1, right, before, after)


def product_of(a, b):
    return a[0] * b[0] - a[1] * b[1], a[0] * b[1] + a[1] * b[0]


def conj_product(a, b):
    return a[0] * b[0] + a[1] * b[1], a[0] * b[1] - a[1] * b[0]


class Place:
    def __init__(self, offs, count, j):
        self.used = j < count[0, 0]
        slot = jnp.where(self.used, j, 0)
        top, left = offs[0, 0, slot, 0], offs[0, 0, slot, 1]
        self.r, self.c = top & 7, left & (H - 1)
        self.row = pl.multiple_of(top - self.r, 8)
        self.wrap = pl.multiple_of(jnp.minimum(self.row + N, 3 * N - 8), 8)
        self.after = pl.multiple_of(self.row + 8, 8)
        tile = lax.shift_right_logical(left, 7)
        self.tiles = tile, tile + 1, jnp.minimum(tile + 2, 5)
        self.rows = lax.broadcasted_iota(jnp.int32, (8, H), 0) >= self.r
        self.cols = lax.broadcasted_iota(jnp.int32, (N, H), 1) >= self.c

    def column(self, tiled, plane, tile):
        first = tiled[plane, tile, pl.ds(self.row, 8), :]
        wrapped = tiled[plane, tile, pl.ds(self.wrap, 8), :]
        rest = tiled[plane, tile, pl.ds(self.after, N - 8), :]
        return jnp.concatenate([jnp.where(self.rows, first, wrapped), rest], 0)

    def take(self, tiled, plane):
        a, b, c = (self.column(tiled, plane, t) for t in self.tiles)
        return jnp.concatenate([jnp.where(self.cols, a, c), b], 1)

    def add(self, tiled, plane, value):
        first, second = value[:, :H], value[:, H:]
        parts = jnp.where(self.cols, first, 0.0), second, jnp.where(self.cols, 0.0, first)
        for tile, part in zip(self.tiles, parts):
            tiled[plane, tile, pl.ds(self.after, N - 8), :] += part[8:]
            tiled[plane, tile, pl.ds(self.row, 8), :] += jnp.where(self.rows, part[:8], 0.0)
            tiled[plane, tile, pl.ds(self.wrap, 8), :] += jnp.where(self.rows, 0.0, part[:8])

    def shifted(self, probe):
        keep = jnp.where(self.used, 1.0, 0.0)
        return tuple(pltpu.roll(pltpu.roll(probe[p], self.r, 0), self.c, 1) * keep for p in range(2))


N_COPIES = 22
QUARTERS = tuple(range(TILE // H))


def fill_pairs(padded, s, k, amp, ph, left, right, above, below, corner_a, corner_b):
    own, upper, lower = pl.ds(H, TILE), pl.ds(0, H), pl.ds(H + TILE, H)
    pairs = [(left.at[:, k], padded.at[:, 0, own, :]), (right.at[:, k], padded.at[:, 5, own, :])]
    for q in QUARTERS:
        lanes = pl.ds(q * H, H)
        pairs.append((amp.at[s, :, lanes], padded.at[0, 1 + q, own, :]))
        pairs.append((ph.at[s, :, lanes], padded.at[1, 1 + q, own, :]))
        pairs.append((above.at[:, s, :, lanes], padded.at[:, 1 + q, upper, :]))
        pairs.append((below.at[:, s, :, lanes], padded.at[:, 1 + q, lower, :]))
    for source, rows in ((corner_a, upper), (corner_b, lower)):
        pairs.append((source.at[:, k, :, pl.ds(0, H)], padded.at[:, 0, rows, :]))
        pairs.append((source.at[:, k, :, pl.ds(H, H)], padded.at[:, 5, rows, :]))
    return pairs


def copies_of(pairs, sems):
    return [pltpu.make_async_copy(a, b, sems.at[i]) for i, (a, b) in enumerate(pairs)]


def start_all(copies):
    for c in copies:
        c.start()


def wait_all(copies):
    for c in copies:
        c.wait()


def drain_pairs(totals, by_columns, centre, top, bottom, left, right):
    own, upper, lower = pl.ds(H, TILE), pl.ds(0, H), pl.ds(H + TILE, H)
    rows = pl.ds(0, 3 * N) if by_columns else own
    pairs = [(totals.at[:, 0, rows, :], left), (totals.at[:, 5, rows, :], right)]
    for q in QUARTERS:
        pairs.append((totals.at[:, 1 + q, own, :], centre.at[:, :, pl.ds(q * H, H)]))
    for q, tile in enumerate(range(1, 5) if by_columns else range(6)):
        pairs.append((totals.at[:, tile, upper, :], top.at[:, :, pl.ds(q * H, H)]))
        pairs.append((totals.at[:, tile, lower, :], bottom.at[:, :, pl.ds(q * H, H)]))
    return pairs


def fold_shapes(planes, by_columns=False):
    shape = lambda *s: jax.ShapeDtypeStruct((planes, *s), F32)
    wide, tall = (TILE, 3 * N) if by_columns else (3 * N, TILE)
    return [shape(TILE, TILE), shape(H, wide), shape(H, wide), shape(tall, H), shape(tall, H)]


ANY = pl.BlockSpec(memory_space=pl.ANY)
SMEM = pl.BlockSpec(memory_space=pltpu.SMEM)
VMEM = pl.BlockSpec(memory_space=pltpu.VMEM)
PER_SLOT = pl.BlockSpec((G, 2, N, N), lambda j: (j, 0, 0, 0))
SLOT_SHAPE = jax.ShapeDtypeStruct((SLOTS, 2, N, N), F32)
PARAMS = pltpu.CompilerParams(dimension_semantics=("arbitrary",))
TILED = lambda planes: pltpu.VMEM((planes, 6, 3 * N, H), F32)


def window_of(padded, place):
    amp, ph = place.take(padded, 0), place.take(padded, 1)
    sine, cosine = sincos(ph)
    return amp * cosine, amp * sine


def intensity(wave):
    return wave[0] * wave[0] + wave[1] * wave[1]


def waves_in(ref):
    return [(ref[g, 0], ref[g, 1]) for g in range(G)]


def put_waves(ref, waves):
    for g, wave in enumerate(waves):
        ref[g, 0], ref[g, 1] = wave


def add_all(places, totals, plane, values):
    for place, value in zip(places, values):
        place.add(totals, plane, value)


def add_grads(places, totals, plane, waves, backs):
    for place, wave, back in zip(places, waves, backs):
        real, imag = conj_product(wave, back)
        place.add(totals, plane, real)
        place.add(totals, plane + 1, imag)


def each(function, *lists):
    return [function(*items) for items in zip(*lists)]


def enter(scalars, sides, probe, prop, prop_t):
    def kernel(offs, count, *rest):
        arrays, (probe, prop, prop_t) = rest[:8], rest[8:11]
        waves, window_ref, parts = rest[11:14], rest[14], rest[15:20]
        padded, totals, sems = rest[20:]
        j = pl.program_id(0)
        fills = [copies_of(fill_pairs(padded.at[s], s, s, *arrays), sems.at[s]) for s in range(2)]
        places = lambda: [Place(offs, count, G * j + g) for g in range(G)]
        forward = lambda now, windows: both_axes(each(product_of, now, windows), prop, prop_t, True, True)

        @pl.when(j == 0)
        def _():
            start_all(fills[0])
            start_all(fills[1])
            totals[...] = jnp.zeros_like(totals)
            wait_all(fills[0])

        @pl.when(G * j < count[0, 0])
        def _():
            at = places()
            now = [place.shifted(probe) for place in at]
            put_waves(waves[0], now)
            add_all(at, totals, 0, each(intensity, now))
            now = forward(now, [window_of(padded.at[0], place) for place in at])
            put_waves(waves[1], now)
            add_all(at, totals, 1, each(intensity, now))

        @pl.when(j == 0)
        def _():
            wait_all(fills[1])

        @pl.when(G * j < count[0, 0])
        def _():
            at = places()
            windows = [window_of(padded.at[1], place) for place in at]
            put_waves(window_ref, windows)
            now = forward(waves_in(waves[1]), windows)
            put_waves(waves[2], now)
            add_all(at, totals, 2, each(intensity, now))

        @pl.when(j == STEPS - 1)
        def _():
            drains = copies_of(drain_pairs(totals, True, *parts), sems.at[0])
            start_all(drains)
            wait_all(drains)

    out = pl.pallas_call(
        kernel,
        name="enter",
        grid=(STEPS,),
        in_specs=[SMEM, SMEM] + [ANY] * 8 + [VMEM] * 3,
        out_specs=[PER_SLOT] * 4 + [ANY] * 5,
        out_shape=[SLOT_SHAPE] * 4 + fold_shapes(3, True),
        scratch_shapes=[pltpu.VMEM((2, 2, 6, 3 * N, H), F32), TILED(3), pltpu.SemaphoreType.DMA((2, N_COPIES))],
        compiler_params=PARAMS,
    )(*scalars, *sides, probe, prop, prop_t)
    return out[:3], out[3], out[4:]


def turn(scalars, sides, incident, target, prop, prop_t, dft, dft_t):
    def kernel(offs, count, *rest):
        arrays, (wave_ref, target_ref, prop, prop_t, dft, dft_t) = rest[:8], rest[8:14]
        back_ref, parts = rest[14], rest[15:20]
        padded, totals, kept_window, kept_wave, sems = rest[20:]
        j = pl.program_id(0)
        fills = [copies_of(fill_pairs(padded.at[k], k + 2, k, *arrays), sems.at[k]) for k in range(2)]
        places = lambda: [Place(offs, count, G * j + g) for g in range(G)]

        @pl.when(j == 0)
        def _():
            start_all(fills[0])
            start_all(fills[1])
            totals[...] = jnp.zeros_like(totals)
            wait_all(fills[0])

        @pl.when(G * j < count[0, 0])
        def _():
            at = places()
            windows = [window_of(padded.at[0], place) for place in at]
            put_waves(kept_window, windows)
            now = both_axes(each(product_of, waves_in(wave_ref), windows), prop, prop_t, True, True)
            put_waves(kept_wave, now)
            add_all(at, totals, 4, each(intensity, now))

        @pl.when(j == 0)
        def _():
            wait_all(fills[1])

        @pl.when(G * j < count[0, 0])
        def _():
            at = places()
            windows = [window_of(padded.at[1], place) for place in at]
            far = both_axes(each(product_of, waves_in(kept_wave), windows), dft, dft_t, True, False)
            misfits = [intensity(wave) - target_ref[g] for g, wave in enumerate(far)]
            scaled = [(misfit * wave[0], misfit * wave[1]) for misfit, wave in zip(misfits, far)]
            backs = both_axes(scaled, dft_t, dft, False, True)
            add_grads(at, totals, 0, waves_in(kept_wave), backs)
            backs = both_axes(each(conj_product, windows, backs), prop_t, prop, True, True)
            add_grads(at, totals, 2, waves_in(wave_ref), backs)
            backs = both_axes(each(conj_product, waves_in(kept_window), backs), prop_t, prop, True, True)
            put_waves(back_ref, backs)

        @pl.when(j == STEPS - 1)
        def _():
            drains = copies_of(drain_pairs(totals, True, *parts), sems.at[0])
            start_all(drains)
            wait_all(drains)

    out = pl.pallas_call(
        kernel,
        name="turn",
        grid=(STEPS,),
        in_specs=[SMEM, SMEM] + [ANY] * 8 + [PER_SLOT, pl.BlockSpec((G, N, N), lambda j: (j, 0, 0))] + [VMEM] * 4,
        out_specs=[PER_SLOT] + [ANY] * 5,
        out_shape=[SLOT_SHAPE] + fold_shapes(5, True),
        scratch_shapes=[
            pltpu.VMEM((2, 2, 6, 3 * N, H), F32),
            TILED(5),
            pltpu.VMEM((G, 2, N, N), F32),
            pltpu.VMEM((G, 2, N, N), F32),
            pltpu.SemaphoreType.DMA((2, N_COPIES)),
        ],
        compiler_params=PARAMS,
    )(*scalars, *sides, incident, target, prop, prop_t, dft, dft_t)
    return out[0], out[1:]


def leave(scalars, incident_0, incident_1, window_1, back, prop, prop_t):
    def kernel(offs, count, wave_0, wave_1, window_ref, back_ref, prop, prop_t, *rest):
        parts, (totals, sems) = rest[:5], rest[5:]
        j = pl.program_id(0)

        @pl.when(j == 0)
        def _():
            totals[...] = jnp.zeros_like(totals)

        @pl.when(G * j < count[0, 0])
        def _():
            at = [Place(offs, count, G * j + g) for g in range(G)]
            backs = waves_in(back_ref)
            add_grads(at, totals, 0, waves_in(wave_1), backs)
            backs = both_axes(each(conj_product, waves_in(window_ref), backs), prop_t, prop, True, True)
            add_grads(at, totals, 2, waves_in(wave_0), backs)

        @pl.when(j == STEPS - 1)
        def _():
            drains = copies_of(drain_pairs(totals, False, *parts), sems)
            start_all(drains)
            wait_all(drains)

    return pl.pallas_call(
        kernel,
        name="leave",
        grid=(STEPS,),
        in_specs=[SMEM, SMEM] + [PER_SLOT] * 4 + [VMEM] * 2,
        out_specs=[ANY] * 5,
        out_shape=fold_shapes(4),
        scratch_shapes=[TILED(4), pltpu.SemaphoreType.DMA((N_COPIES,))],
        compiler_params=PARAMS,
    )(*scalars, incident_0, incident_1, window_1, back, prop, prop_t)


def reorder_targets(measured):
    def kernel(m_ref, o_ref):
        r = lax.broadcasted_iota(jnp.int32, (N, N), 0)
        c = lax.broadcasted_iota(jnp.int32, (N, N), 1)

        def one_hot(to, source):
            return jnp.where(source == jnp.where(to < H, 2 * to, 2 * to - (N - 1)), 1.0, 0.0).astype(BF16)

        def thirds(x):
            a = x.astype(BF16)
            rest = x - a.astype(F32)
            b = rest.astype(BF16)
            return a, b, (rest - b.astype(F32)).astype(BF16)

        rows, cols = one_hot(r, c), one_hot(c, r)
        a, b, d = thirds(m_ref[0, 0, 0])
        x = (dot(rows, a) + dot(rows, b)) + dot(rows, d)
        a, b, d = thirds(x)
        o_ref[0] = (dot(a, cols) + dot(b, cols)) + dot(d, cols)

    return pl.pallas_call(
        kernel,
        name="reorder",
        grid=(SLOTS,),
        in_specs=[pl.BlockSpec((1, 1, 1, N, N), lambda j: (0, 0, j, 0, 0))],
        out_specs=pl.BlockSpec((1, N, N), lambda j: (j, 0, 0)),
        out_shape=jax.ShapeDtypeStruct((SLOTS, N, N), F32),
        compiler_params=PARAMS,
    )(measured)


def rims_with_rows(parts, from_above, from_below):
    left, right = parts[3:]
    planes = left.shape[0]

    def kernel(l_ref, r_ref, fal, far, fbl, fbr, lo, ro):
        for source, out, fa, fb in ((l_ref, lo, fal, fbl), (r_ref, ro, far, fbr)):
            out[:, :H, :] = source[:, :H, :] + fa[...]
            out[:, H:TILE - H, :] = source[:, H:TILE - H, :]
            out[:, TILE - H:, :] = source[:, TILE - H:, :] + fb[...]

    whole = pl.BlockSpec((planes, TILE, H), lambda i: (0, 0, 0))
    ends = [pl.BlockSpec((planes, H, H), lambda i: (0, 0, 0)), pl.BlockSpec((planes, H, H), lambda i: (0, 0, 5))]
    return pl.pallas_call(
        kernel,
        grid=(1,),
        in_specs=[whole] * 2 + ends * 2,
        out_specs=[whole] * 2,
        out_shape=[jax.ShapeDtypeStruct((planes, TILE, H), F32)] * 2,
    )(left, right, from_above, from_above, from_below, from_below)


def rims_with_columns(parts, from_left, from_right):
    top, bottom = parts[1:3]
    planes = top.shape[0]

    def kernel(t_ref, b_ref, flt, flb, frt, frb, to, bo):
        for source, out, fl, fr in ((t_ref, to, flt, frt), (b_ref, bo, flb, frb)):
            out[:, :, :H] = source[:, :, :H] + fl[...]
            out[:, :, H:TILE - H] = source[:, :, H:TILE - H]
            out[:, :, TILE - H:] = source[:, :, TILE - H:] + fr[...]

    whole = pl.BlockSpec((planes, H, TILE), lambda i: (0, 0, 0))
    ends = [pl.BlockSpec((planes, H, H), lambda i: (0, 0, 0)), pl.BlockSpec((planes, H, H), lambda i: (0, 5, 0))]
    return pl.pallas_call(
        kernel,
        grid=(1,),
        in_specs=[whole] * 2 + ends * 2,
        out_specs=[whole] * 2,
        out_shape=[jax.ShapeDtypeStruct((planes, H, TILE), F32)] * 2,
    )(top, bottom, from_left, from_left, from_right, from_right)


def shifted(value, axis, steps):
    count = lax.axis_size(axis)
    leading, last = max(0, -steps), min(count, count - steps)
    return lax.ppermute(value, axis, [(source, source + steps) for source in range(leading, last)])


def light_scale(plane, planes, centre, from_left, from_right, from_above, from_below):
    blocks = TILE // H
    at = plane // planes

    def kernel(centre, left, right, above, below, out):
        c = pl.program_id(0)
        out[...] = centre[...]
        out[:, :H, :] += above[...]
        out[:, TILE - H:, :] += below[...]

        @pl.when(c == 0)
        def _():
            out[...] += left[:, H:H + TILE, :]

        @pl.when(c == blocks - 1)
        def _():
            out[...] += right[:, H:H + TILE, :]

        out[...] = 1.0 / (out[...] + 1.0)

    column = pl.BlockSpec((planes, TILE, H), lambda c: (at, 0, c))
    side = pl.BlockSpec((planes, 3 * N, H), lambda c: (at, 0, 0))
    end = pl.BlockSpec((planes, H, H), lambda c: (at, 0, c))
    return pl.pallas_call(
        kernel,
        grid=(blocks,),
        in_specs=[column, side, side, end, end],
        out_specs=pl.BlockSpec((planes, TILE, H), lambda c: (0, 0, c)),
        out_shape=jax.ShapeDtypeStruct((planes, TILE, TILE), F32),
        compiler_params=PARAMS,
    )(centre, from_left, from_right, from_above, from_below)


OUT_SHAPE = [jax.ShapeDtypeStruct((SLICES, TILE, TILE), F32)] * 2
PARAMS_2 = pltpu.CompilerParams(dimension_semantics=("arbitrary", "arbitrary"))


def update(slices, first, amp, ph, centre, above, below, sides, scale, scale_of, previous):
    last = TILE // H - 1
    top_slice = slices[0]
    across = sides is None
    here = pl.BlockSpec((1, TILE, H), lambda a, c: (top_slice - a, 0, c))
    end = pl.BlockSpec((2, H, H), lambda a, c: (first + a, 0, c + (1 if across else 0)))
    operands = [amp, ph, centre, above, below, scale]
    specs = [here, here, pl.BlockSpec((2, TILE, H), lambda a, c: (first + a, 0, c)), end, end]
    specs.append(pl.BlockSpec((1, TILE, H), lambda a, c: (top_slice - a - scale_of, 0, c)))
    if sides:
        operands += list(sides)
        specs += [pl.BlockSpec((2, 3 * N, H), lambda a, c: (first + a, 0, 0))] * 2
    used = len(operands)
    if previous:
        operands += list(previous)
        specs += [ANY] * 2

    def kernel(*refs):
        amp_ref, ph_ref, centre, above, below, scale = refs[:6]
        out_r, out_i = refs[-2:]
        c = pl.program_id(1)

        def total(p):
            x = centre[p]
            x = jnp.concatenate([x[:H] + above[p], x[H:TILE - H], x[TILE - H:] + below[p]], 0)
            if sides:
                left, right = refs[6][p, H:H + TILE, :], refs[7][p, H:H + TILE, :]
                x = x + jnp.where(c == 0, left, jnp.where(c == last, right, 0.0))
            return x

        sine, cosine = sincos(ph_ref[0])
        out_r[0] = amp_ref[0] * cosine - total(0) * scale[0]
        out_i[0] = amp_ref[0] * sine - total(1) * scale[0]

    return pl.pallas_call(
        kernel,
        grid=(len(slices), TILE // H),
        in_specs=specs,
        out_specs=[here, here],
        out_shape=OUT_SHAPE,
        input_output_aliases={used: 0, used + 1: 1} if previous else {},
        compiler_params=PARAMS_2,
    )(*operands)


def finish(outs, sides, scale):
    def kernel(left, right, scale, in_r, in_i, out_r, out_i):
        c = pl.program_id(1)
        for p, (source, out) in enumerate(((in_r, out_r), (in_i, out_i))):
            out[0] = source[0] - jnp.where(c == 0, left[p], right[p]) * scale[0]

    here = pl.BlockSpec((1, TILE, H), lambda a, c: (1 - a, 0, 3 * c))
    side = pl.BlockSpec((2, TILE, H), lambda a, c: (a, 0, 0))
    return pl.pallas_call(
        kernel,
        name="finish",
        grid=(2, 2),
        in_specs=[side, side, here, here, here],
        out_specs=[here, here],
        out_shape=OUT_SHAPE,
        input_output_aliases={3: 0, 4: 1},
        compiler_params=PARAMS_2,
    )(*sides, scale, *outs)


def program(object_amp, object_phase, probe_field, measured, offsets, counts):
    prop, dft = lax.optimization_barrier(tuple(jnp.asarray(t) for t in tables()))
    prop_t, dft_t = jnp.swapaxes(prop, 2, 3), jnp.swapaxes(dft, 2, 3)
    amp, ph = object_amp, object_phase
    scalars = (offsets, counts)
    edges = []
    for a, b in ((0, 2), (2, 4)):
        edge = lambda cols: jnp.stack([amp[a:b, :, cols], ph[a:b, :, cols]])
        left = shifted(edge(slice(TILE - H, TILE)), "col", 1)
        right = shifted(edge(slice(0, H)), "col", -1)
        edges.append((left, right))
    above = shifted(jnp.stack([amp[:, TILE - H:], ph[:, TILE - H:]]), "row", 1)
    below = shifted(jnp.stack([amp[:, :H], ph[:, :H]]), "row", -1)
    sides = []
    for left, right in edges:
        corner = lambda rows: jnp.concatenate([left[:, :, rows], right[:, :, rows]], 3)
        corner_a = shifted(corner(slice(TILE - H, TILE)), "row", 1)
        corner_b = shifted(corner(slice(0, H)), "row", -1)
        sides.append((amp, ph, left, right, above, below, corner_a, corner_b))
    target = reorder_targets(measured)

    waves, window_1, lights = enter(scalars, sides[0], probe_field, prop, prop_t)
    light_left = shifted(lights[4], "col", 1)
    light_right = shifted(lights[3], "col", -1)

    back, grads_a = turn(scalars, sides[1], waves[2], target, prop, prop_t, dft, dft_t)
    a_left = shifted(grads_a[4], "col", 1)
    a_right = shifted(grads_a[3], "col", -1)

    grads_b = leave(scalars, waves[0], waves[1], window_1, back, prop, prop_t)
    b_above = shifted(grads_b[2], "row", 1)
    b_below = shifted(grads_b[1], "row", -1)

    to_up, to_down = rims_with_columns(lights, light_left, light_right)
    light_above = shifted(to_down, "row", 1)
    light_below = shifted(to_up, "row", -1)
    scale = light_scale(0, 3, lights[0], light_left, light_right, light_above, light_below)

    to_left, to_right = rims_with_rows(grads_b, b_above, b_below)
    b_sides = shifted(to_right, "col", 1), shifted(to_left, "col", -1)

    to_up, to_down = rims_with_columns(grads_a, a_left, a_right)
    a_above = shifted(to_down, "row", 1)
    a_below = shifted(to_up, "row", -1)
    scale_3 = light_scale(4, 1, grads_a[0], a_left, a_right, a_above, a_below)

    a_parts = (grads_a[0], a_above, a_below, (a_left, a_right))
    outs = update((1, 0), 0, amp, ph, grads_b[0], b_above, b_below, None, scale, 0, None)
    outs = update((3,), 0, amp, ph, *a_parts, scale_3, 3, outs)
    outs = update((2,), 1, amp, ph, *a_parts, scale, 0, outs)
    return tuple(finish(outs, b_sides, scale))


def solution(mesh):
    placed = (
        P(None, "row", "col"),
        P(None, "row", "col"),
        P(),
        P("row", "col", None, None, None),
        P("row", "col", None, None),
        P("row", "col"),
    )
    return jax.shard_map(
        program,
        mesh=mesh,
        in_specs=placed,
        out_specs=(P(None, "row", "col"), P(None, "row", "col")),
        check_vma=False,
    )
```
